32 devices in a mesh: band: 2 (over y), row: 16 (over z, x, core).
Axes of the slice: x: 2, y: 2, z: 4, core: 2. Of those that a mesh axis runs over, the one named last changes fastest.
Arguments:
- coeffs: bfloat16 [2, 6144, 4096], P(None, 'row', 'band'), may hold values from -6 to 6
- rotation: bfloat16 [2, 4096, 4096], P(None, 'row', 'band'), may hold values from -0.0625 to 0.0625
Outputs:
- rotated: bfloat16 [2, 6144, 4096], P(None, 'row', 'band')
The draws below stay inside these ranges and needn't reach their ends.
All inputs are finite; a program needn't handle non-finite values.
Results may differ from the reference program's by a relative error of at most 0.0014.
Values may be sent and summed in bfloat16 or wider, within the bound.
A program may use at most 128 MiB of HBM per device.

```python
import jax
import jax.numpy as jnp
from jax import lax

NB = 4096
ROWS = 6144


def block_scale(own_key, dims, split, low, top_value):
    def one(dim, blocks):
        heights = jax.random.uniform(jax.random.fold_in(jax.random.fold_in(own_key, 6), dim), (blocks,), jnp.float32, low / len(split), top_value / len(split))
        return jnp.repeat(jnp.exp(heights), dims[dim] // blocks).reshape((-1,) + (1,) * (len(dims) - dim - 1))

    factor_of = one(*split[0])
    for cut in split[1:]:
        factor_of = factor_of * one(*cut)
    return factor_of


def gaussian(key, shape, deviation, bound, shards=(), dtype=jnp.bfloat16):
    drawn = jax.random.normal(key, shape, jnp.float32) * deviation
    if len(shards) > 0:
        drawn = block_scale(key, shape, shards, -0.22, 0.18) * drawn
    return jnp.clip(drawn, min=-bound, max=bound).astype(dtype)


def setup_inputs(seed: int = 0) -> dict:
    key_of = jax.random.split(jax.random.key(seed), 3)
    coeffs = gaussian(key_of[0], (2, ROWS, NB), 1.0, 6.0, ((1, 16), (2, 2)))
    rotation = gaussian(key_of[1], (2, NB, NB), (2 * NB) ** -0.5, 0.0625, ((1, 16), (2, 2)))
    return {"coeffs": coeffs, "rotation": rotation}


def reference(coeffs, rotation):
    real_c = coeffs[0].astype(jnp.float32)
    imag_c = coeffs[1].astype(jnp.float32)
    real_q = rotation[0].astype(jnp.float32)
    imag_q = rotation[1].astype(jnp.float32)
    high = lax.Precision.HIGHEST
    real_out = jnp.dot(real_c, real_q, precision=high, preferred_element_type=jnp.float32) - jnp.dot(imag_c, imag_q, precision=high, preferred_element_type=jnp.float32)
    imag_out = jnp.dot(real_c, imag_q, precision=high, preferred_element_type=jnp.float32) + jnp.dot(imag_c, real_q, precision=high, preferred_element_type=jnp.float32)
    return jnp.stack([real_out, imag_out]).astype(jnp.bfloat16)
```

```python
import jax
import jax.numpy as jnp
from jax import lax
from jax.sharding import PartitionSpec as P

CHUNKS = 4


def complex_product(left, right):
    real_out = jnp.dot(left[0], right[0], preferred_element_type=jnp.float32) - jnp.dot(
        left[1], right[1], preferred_element_type=jnp.float32
    )
    imag_out = jnp.dot(left[0], right[1], preferred_element_type=jnp.float32) + jnp.dot(
        left[1], right[0], preferred_element_type=jnp.float32
    )
    return jnp.stack([real_out, imag_out])


def solution(mesh):
    bands = mesh.shape["band"]

    def body(coeffs, rotation):
        me = lax.axis_index("band")
        width = coeffs.shape[2]
        whole = jnp.zeros(coeffs.shape[:2] + (width * bands,), coeffs.dtype)
        whole = lax.dynamic_update_slice_in_dim(whole, coeffs, me * width, 2)
        for step in range(1, bands):
            perm = [(i, (i + step) % bands) for i in range(bands)]
            block = lax.ppermute(coeffs, "band", perm)
            owner = lax.rem(me - step + bands, bands)
            whole = lax.dynamic_update_slice_in_dim(whole, block, owner * width, 2)
        columns = rotation.shape[2] // CHUNKS
        outs = []
        for chunk in range(CHUNKS):
            piece = rotation[:, :, chunk * columns : (chunk + 1) * columns]
            gathered = lax.all_gather(piece, "row", axis=1, tiled=True)
            outs.append(complex_product(whole, gathered).astype(jnp.bfloat16))
        return jnp.concatenate(outs, axis=2)

    in_specs = (P(None, "row", "band"), P(None, "row", "band"))
    out_specs = P(None, "row", "band")
    return jax.shard_map(body, mesh=mesh, in_specs=in_specs, out_specs=out_specs, check_vma=False)
```

```python
import jax
import jax.numpy as jnp
from jax import lax
from jax.sharding import PartitionSpec as P

CHUNKS = 1


def complex_product(left, right):
    real_out = jnp.dot(left[0], right[0], preferred_element_type=jnp.float32) - jnp.dot(
        left[1], right[1], preferred_element_type=jnp.float32
    )
    imag_out = jnp.dot(left[0], right[1], preferred_element_type=jnp.float32) + jnp.dot(
        left[1], right[0], preferred_element_type=jnp.float32
    )
    return jnp.stack([real_out, imag_out])


def solution(mesh):
    bands = mesh.shape["band"]

    def body(coeffs, rotation):
        me = lax.axis_index("band")
        width = coeffs.shape[2]
        whole = jnp.zeros(coeffs.shape[:2] + (width * bands,), coeffs.dtype)
        whole = lax.dynamic_update_slice_in_dim(whole, coeffs, me * width, 2)
        for step in range(1, bands):
            perm = [(i, (i + step) % bands) for i in range(bands)]
            block = lax.ppermute(coeffs, "band", perm)
            owner = lax.rem(me - step + bands, bands)
            whole = lax.dynamic_update_slice_in_dim(whole, block, owner * width, 2)
        columns = rotation.shape[2] // CHUNKS
        outs = []
        for chunk in range(CHUNKS):
            piece = rotation[:, :, chunk * columns : (chunk + 1) * columns]
            gathered = lax.all_gather(piece, "row", axis=1, tiled=True)
            outs.append(complex_product(whole, gathered).astype(jnp.bfloat16))
        return jnp.concatenate(outs, axis=2)

    in_specs = (P(None, "row", "band"), P(None, "row", "band"))
    out_specs = P(None, "row", "band")
    return jax.shard_map(body, mesh=mesh, in_specs=in_specs, out_specs=out_specs, check_vma=False)
```

```python
import functools

import jax
import jax.numpy as jnp
from jax import lax
from jax.experimental import pallas as pl
from jax.experimental.pallas import tpu as pltpu
from jax.sharding import PartitionSpec as P

MESH = pl.DeviceIdType.MESH
CORES = 2
SUBS = 2


def kernel(chips, bands, tile, coeffs_ref, rotation_ref, out_ref, held, whole, total,
           ring_send, ring_recv, pair_send, pair_recv, band_send, band_recv, own_sem):
    band = lax.axis_index("band")
    row = lax.axis_index("row")
    depth = rotation_ref.shape[1]
    columns = rotation_ref.shape[2]
    width = coeffs_ref.shape[2]
    sub = depth // SUBS
    half = chips // 2

    chip = row // CORES
    core = row % CORES
    line = chip // 2
    side = chip % 2
    place = line + side * (chips - 1 - 2 * line)

    def chip_at(position):
        back = position // half
        return (1 - back) * 2 * position + back * (2 * (chips - 1 - position) + 1)

    ahead = chip_at((place + 1) % chips) * CORES + core
    behind = chip_at((place + chips - 1) % chips) * CORES + core
    sibling = chip * CORES + (1 - core)
    partners = [(band + step) % bands for step in range(1, bands)]

    barrier = pltpu.get_barrier_semaphore()
    for other in (ahead, behind, sibling):
        pl.semaphore_signal(barrier, inc=1, device_id={"row": other}, device_id_type=MESH)
    for other in partners:
        pl.semaphore_signal(barrier, inc=1, device_id={"band": other}, device_id_type=MESH)
    pl.semaphore_wait(barrier, 3 + len(partners))

    def mine(part, step, piece):
        start = pl.multiple_of(core * depth + piece * sub, sub)
        return held.at[part, step, pl.ds(start, sub)]

    def source(part, step, piece):
        if step == 0:
            return rotation_ref.at[part, pl.ds(piece * sub, sub)]
        return mine(part, step, piece)

    def hop(part, step, piece):
        return pltpu.make_async_remote_copy(
            src_ref=source(part, step, piece),
            dst_ref=mine(part, step + 1, piece),
            send_sem=ring_send.at[part, step, piece],
            recv_sem=ring_recv.at[part, step, piece],
            device_id={"row": (ahead, behind)[part]},
            device_id_type=MESH,
        )

    def share(part, step, piece):
        return pltpu.make_async_remote_copy(
            src_ref=source(part, step, piece),
            dst_ref=mine(part, step, piece),
            send_sem=pair_send.at[part, step, piece],
            recv_sem=pair_recv.at[part, step, piece],
            device_id={"row": sibling},
            device_id_type=MESH,
        )

    pieces = [(part, piece) for piece in range(SUBS) for part in range(2)]
    for part, piece in pieces:
        hop(part, 0, piece).start()
    spread = [
        pltpu.make_async_remote_copy(
            src_ref=coeffs_ref,
            dst_ref=whole.at[band],
            send_sem=band_send.at[i],
            recv_sem=band_recv.at[i],
            device_id={"band": other},
            device_id_type=MESH,
        )
        for i, other in enumerate(partners)
    ]
    for copy in spread:
        copy.start()
    for part, piece in pieces:
        share(part, 0, piece).start()
    own = [pltpu.make_async_copy(coeffs_ref, whole.at[band], own_sem.at[0])]
    for part in range(2):
        start = pl.multiple_of(core * depth, depth)
        own.append(
            pltpu.make_async_copy(rotation_ref.at[part], held.at[part, 0, pl.ds(start, depth)], own_sem.at[1 + part])
        )
    for copy in own:
        copy.start()
    for copy in own:
        copy.wait()

    def multiply(step):
        for part, piece in pieces:
            share(part, step, piece).wait_recv()
        spans = []
        for origin in ((place + chips - step) % chips, (place + step) % chips):
            first = chip_at(origin) * (CORES * depth)
            spans.append((first // width, pl.multiple_of(first % width, CORES * depth)))

        def left(part, span):
            return whole[span[0], part, :, pl.ds(span[1], CORES * depth)]

        @pl.loop(0, columns // tile)
        def _(i):
            cut = pl.ds(pl.multiple_of(i * tile, tile), tile)
            real = held[0, step, :, cut]
            imag = held[1, step, :, cut]
            dot = functools.partial(jnp.dot, preferred_element_type=jnp.float32)
            real_term = dot(left(0, spans[0]), real) - dot(left(1, spans[1]), imag)
            if step > 0:
                real_term += total[0, :, cut]
            imag_term = dot(left(1, spans[0]), real) + dot(left(0, spans[1]), imag)
            if step > 0:
                imag_term += total[1, :, cut]
            if step < chips - 1:
                total[0, :, cut] = real_term
                total[1, :, cut] = imag_term
            else:
                out_ref[0, :, cut] = real_term.astype(out_ref.dtype)
                out_ref[1, :, cut] = imag_term.astype(out_ref.dtype)

    events = (chips - 1) * SUBS
    event = 0
    for step in range(1, chips):
        for piece in range(SUBS):
            for part in range(2):
                hop(part, step - 1, piece).wait_recv()
                if step < chips - 1:
                    hop(part, step, piece).start()
                share(part, step, piece).start()
            ready = event - (events - chips)
            if ready == 0:
                for copy in spread:
                    copy.wait_recv()
            if ready >= 0:
                multiply(ready)
            event += 1

    for copy in spread:
        copy.wait_send()
    for step in range(chips):
        for part, piece in pieces:
            if step < chips - 1:
                hop(part, step, piece).wait_send()
            share(part, step, piece).wait_send()


def solution(mesh):
    bands, rows = mesh.shape["band"], mesh.shape["row"]
    chips = rows // CORES

    def body(coeffs, rotation):
        depth, columns = rotation.shape[1:]
        tile = min(256, columns)
        return pl.pallas_call(
            functools.partial(kernel, chips, bands, tile),
            out_shape=jax.ShapeDtypeStruct(coeffs.shape, jnp.bfloat16),
            in_specs=[pl.BlockSpec(memory_space=pl.ANY)] * 2,
            out_specs=pl.BlockSpec(memory_space=pltpu.VMEM),
            scratch_shapes=[
                pltpu.VMEM((2, chips, CORES * depth, columns), jnp.bfloat16),
                pltpu.VMEM((bands,) + coeffs.shape, jnp.bfloat16),
                pltpu.VMEM(coeffs.shape, jnp.float32),
                pltpu.SemaphoreType.DMA((2, chips - 1, SUBS)),
                pltpu.SemaphoreType.DMA((2, chips - 1, SUBS)),
                pltpu.SemaphoreType.DMA((2, chips, SUBS)),
                pltpu.SemaphoreType.DMA((2, chips, SUBS)),
                pltpu.SemaphoreType.DMA((bands - 1,)),
                pltpu.SemaphoreType.DMA((bands - 1,)),
                pltpu.SemaphoreType.DMA((3,)),
            ],
            compiler_params=pltpu.CompilerParams(
                collective_id=0, has_side_effects=True, vmem_limit_bytes=62 * 1024 * 1024
            ),
        )(coeffs, rotation)

    in_specs = (P(None, "row", "band"), P(None, "row", "band"))
    out_specs = P(None, "row", "band")
    return jax.shard_map(body, mesh=mesh, in_specs=in_specs, out_specs=out_specs, check_vma=False)
```

```python
import functools

import jax
import jax.numpy as jnp
from jax import lax
from jax.experimental import pallas as pl
from jax.experimental.pallas import tpu as pltpu
from jax.sharding import PartitionSpec as P

MESH = pl.DeviceIdType.MESH
CORES = 2
PIECE_BYTES = 256 * 1024


def kernel(chips, bands, cuts, tile, coeffs_ref, rotation_ref, out_ref, held, whole, total,
           ring_send, ring_recv, pair_send, pair_recv, band_send, band_recv, own_sem):
    band = lax.axis_index("band")
    row = lax.axis_index("row")
    depth = rotation_ref.shape[1]
    columns = rotation_ref.shape[2] // cuts
    width = coeffs_ref.shape[2]
    half = chips // 2

    chip = row // CORES
    core = row % CORES
    line = chip // 2
    side = chip % 2
    place = line + side * (chips - 1 - 2 * line)

    def chip_at(position):
        back = position // half
        return (1 - back) * 2 * position + back * (2 * (chips - 1 - position) + 1)

    ahead = chip_at((place + 1) % chips) * CORES + core
    behind = chip_at((place + chips - 1) % chips) * CORES + core
    sibling = chip * CORES + (1 - core)
    partners = [(band + step) % bands for step in range(1, bands)]

    barrier = pltpu.get_barrier_semaphore()
    for other in (ahead, behind, sibling):
        pl.semaphore_signal(barrier, inc=1, device_id={"row": other}, device_id_type=MESH)
    for other in partners:
        pl.semaphore_signal(barrier, inc=1, device_id={"band": other}, device_id_type=MESH)
    pl.semaphore_wait(barrier, 3 + len(partners))

    def mine(part, step, piece):
        return held.at[part, step, piece, pl.ds(pl.multiple_of(core * depth, depth), depth)]

    def source(part, step, piece):
        if step == 0:
            return rotation_ref.at[part, :, pl.ds(piece * columns, columns)]
        return mine(part, step, piece)

    def hop(part, step, piece):
        return pltpu.make_async_remote_copy(
            src_ref=source(part, step, piece),
            dst_ref=mine(part, step + 1, piece),
            send_sem=ring_send.at[part, step, piece],
            recv_sem=ring_recv.at[part, step, piece],
            device_id={"row": (ahead, behind)[part]},
            device_id_type=MESH,
        )

    def share(part, step, piece):
        return pltpu.make_async_remote_copy(
            src_ref=source(part, step, piece),
            dst_ref=mine(part, step, piece),
            send_sem=pair_send.at[part, step, piece],
            recv_sem=pair_recv.at[part, step, piece],
            device_id={"row": sibling},
            device_id_type=MESH,
        )

    pieces = [(part, piece) for piece in range(cuts) for part in range(2)]
    for part, piece in pieces:
        hop(part, 0, piece).start()
    spread = [
        pltpu.make_async_remote_copy(
            src_ref=coeffs_ref,
            dst_ref=whole.at[band],
            send_sem=band_send.at[i],
            recv_sem=band_recv.at[i],
            device_id={"band": other},
            device_id_type=MESH,
        )
        for i, other in enumerate(partners)
    ]
    for copy in spread:
        copy.start()
    for part, piece in pieces:
        share(part, 0, piece).start()
    own = [pltpu.make_async_copy(coeffs_ref, whole.at[band], own_sem.at[0])]
    for i, (part, piece) in enumerate(pieces):
        own.append(pltpu.make_async_copy(source(part, 0, piece), mine(part, 0, piece), own_sem.at[1 + i]))
    for copy in own:
        copy.start()
    for copy in own:
        copy.wait()

    def multiply(step, piece):
        for part in range(2):
            share(part, step, piece).wait_recv()
        spans = []
        for origin in ((place + chips - step) % chips, (place + step) % chips):
            first = chip_at(origin) * (CORES * depth)
            spans.append((first // width, pl.multiple_of(first % width, CORES * depth)))

        def left(part, span):
            return whole[span[0], part, :, pl.ds(span[1], CORES * depth)]

        @pl.loop(0, columns // tile)
        def _(i):
            cut = pl.ds(pl.multiple_of(i * tile, tile), tile)
            out = pl.ds(pl.multiple_of(piece * columns + i * tile, tile), tile)
            real = held[0, step, piece, :, cut]
            imag = held[1, step, piece, :, cut]
            dot = functools.partial(jnp.dot, preferred_element_type=jnp.float32)
            real_term = dot(left(0, spans[0]), real) - dot(left(1, spans[1]), imag)
            if step > 0:
                real_term += total[0, :, out]
            imag_term = dot(left(1, spans[0]), real) + dot(left(0, spans[1]), imag)
            if step > 0:
                imag_term += total[1, :, out]
            if step < chips - 1:
                total[0, :, out] = real_term
                total[1, :, out] = imag_term
            else:
                out_ref[0, :, out] = real_term.astype(out_ref.dtype)
                out_ref[1, :, out] = imag_term.astype(out_ref.dtype)

    units = [(step, piece) for step in range(chips) for piece in range(cuts)]
    events = (chips - 1) * cuts
    begin = events // 2
    done = 0
    for event in range(events):
        step, piece = 1 + event // cuts, event % cuts
        for part in range(2):
            hop(part, step - 1, piece).wait_recv()
            if step < chips - 1:
                hop(part, step, piece).start()
            share(part, step, piece).start()
        if event == begin:
            for copy in spread:
                copy.wait_recv()
        if event >= begin:
            goal = min(event + cuts, 3 * (event - begin + 1))
            for unit in units[done:goal]:
                multiply(*unit)
            done = max(done, goal)
    for unit in units[done:]:
        multiply(*unit)

    for copy in spread:
        copy.wait_send()
    for step in range(chips):
        for part, piece in pieces:
            if step < chips - 1:
                hop(part, step, piece).wait_send()
            share(part, step, piece).wait_send()


def solution(mesh):
    bands, rows = mesh.shape["band"], mesh.shape["row"]
    chips = rows // CORES

    def body(coeffs, rotation):
        depth, columns = rotation.shape[1:]
        cuts = max(1, min(4, depth * columns * 2 // PIECE_BYTES))
        tile = min(256, columns // cuts)
        return pl.pallas_call(
            functools.partial(kernel, chips, bands, cuts, tile),
            out_shape=jax.ShapeDtypeStruct(coeffs.shape, jnp.bfloat16),
            in_specs=[pl.BlockSpec(memory_space=pl.ANY)] * 2,
            out_specs=pl.BlockSpec(memory_space=pltpu.VMEM),
            scratch_shapes=[
                pltpu.VMEM((2, chips, cuts, CORES * depth, columns // cuts), jnp.bfloat16),
                pltpu.VMEM((bands,) + coeffs.shape, jnp.bfloat16),
                pltpu.VMEM(coeffs.shape, jnp.float32),
                pltpu.SemaphoreType.DMA((2, chips - 1, cuts)),
                pltpu.SemaphoreType.DMA((2, chips - 1, cuts)),
                pltpu.SemaphoreType.DMA((2, chips, cuts)),
                pltpu.SemaphoreType.DMA((2, chips, cuts)),
                pltpu.SemaphoreType.DMA((bands - 1,)),
                pltpu.SemaphoreType.DMA((bands - 1,)),
                pltpu.SemaphoreType.DMA((1 + 2 * cuts,)),
            ],
            compiler_params=pltpu.CompilerParams(
                collective_id=0, has_side_effects=True, vmem_limit_bytes=54 * 1024 * 1024
            ),
        )(coeffs, rotation)

    in_specs = (P(None, "row", "band"), P(None, "row", "band"))
    out_specs = P(None, "row", "band")
    return jax.shard_map(body, mesh=mesh, in_specs=in_specs, out_specs=out_specs, check_vma=False)
```

```python
import functools

import jax
import jax.numpy as jnp
from jax import lax
from jax.experimental import pallas as pl
from jax.experimental.pallas import tpu as pltpu
from jax.sharding import PartitionSpec as P

MESH = pl.DeviceIdType.MESH
CORES = 2
PIECE_BYTES = 256 * 1024


def kernel(chips, bands, cuts, tile, coeffs_ref, rotation_ref, out_ref, held, whole, total,
           ring_send, ring_recv, pair_send, pair_recv, band_send, band_recv, own_sem):
    band = lax.axis_index("band")
    row = lax.axis_index("row")
    depth = rotation_ref.shape[1]
    columns = rotation_ref.shape[2] // cuts
    width = coeffs_ref.shape[2]
    half = chips // 2

    chip = row // CORES
    core = row % CORES
    line = chip // 2
    side = chip % 2
    place = line + side * (chips - 1 - 2 * line)

    def chip_at(position):
        back = position // half
        return (1 - back) * 2 * position + back * (2 * (chips - 1 - position) + 1)

    ahead = chip_at((place + 1) % chips) * CORES + core
    behind = chip_at((place + chips - 1) % chips) * CORES + core
    sibling = chip * CORES + (1 - core)
    partners = [(band + step) % bands for step in range(1, bands)]

    barrier = pltpu.get_barrier_semaphore()
    for other in (ahead, behind, sibling):
        pl.semaphore_signal(barrier, inc=1, device_id={"row": other}, device_id_type=MESH)
    for other in partners:
        pl.semaphore_signal(barrier, inc=1, device_id={"band": other}, device_id_type=MESH)
    pl.semaphore_wait(barrier, 3 + len(partners))

    def mine(part, step, piece):
        return held.at[part, step, piece, pl.ds(pl.multiple_of(core * depth, depth), depth)]

    def source(part, step, piece):
        if step == 0:
            return rotation_ref.at[part, :, pl.ds(piece * columns, columns)]
        return mine(part, step, piece)

    def hop(part, step, piece):
        return pltpu.make_async_remote_copy(
            src_ref=source(part, step, piece),
            dst_ref=mine(part, step + 1, piece),
            send_sem=ring_send.at[part, step, piece],
            recv_sem=ring_recv.at[part, step, piece],
            device_id={"row": (ahead, behind)[part]},
            device_id_type=MESH,
        )

    def share(part, step, piece):
        return pltpu.make_async_remote_copy(
            src_ref=source(part, step, piece),
            dst_ref=mine(part, step, piece),
            send_sem=pair_send.at[part, step, piece],
            recv_sem=pair_recv.at[part, step, piece],
            device_id={"row": sibling},
            device_id_type=MESH,
        )

    pieces = [(part, piece) for piece in range(cuts) for part in range(2)]
    for part, piece in pieces:
        hop(part, 0, piece).start()
    spread = [
        pltpu.make_async_remote_copy(
            src_ref=coeffs_ref,
            dst_ref=whole.at[band],
            send_sem=band_send.at[i],
            recv_sem=band_recv.at[i],
            device_id={"band": other},
            device_id_type=MESH,
        )
        for i, other in enumerate(partners)
    ]
    for copy in spread:
        copy.start()
    for part, piece in pieces:
        share(part, 0, piece).start()
    own = [pltpu.make_async_copy(coeffs_ref, whole.at[band], own_sem.at[0])]
    for i, (part, piece) in enumerate(pieces):
        own.append(pltpu.make_async_copy(source(part, 0, piece), mine(part, 0, piece), own_sem.at[1 + i]))
    for copy in own:
        copy.start()
    for copy in own:
        copy.wait()

    def multiply(step, piece):
        for part in range(2):
            share(part, step, piece).wait_recv()
        spans = []
        for origin in ((place + chips - step) % chips, (place + step) % chips):
            first = chip_at(origin) * (CORES * depth)
            spans.append((first // width, pl.multiple_of(first % width, CORES * depth)))

        def left(part, span):
            return whole[span[0], part, :, pl.ds(span[1], CORES * depth)]

        @pl.loop(0, columns // tile)
        def _(i):
            cut = pl.ds(pl.multiple_of(i * tile, tile), tile)
            out = pl.ds(pl.multiple_of(piece * columns + i * tile, tile), tile)
            real = held[0, step, piece, :, cut]
            imag = held[1, step, piece, :, cut]
            dot = functools.partial(jnp.dot, preferred_element_type=jnp.float32)
            real_term = dot(left(0, spans[0]), real) - dot(left(1, spans[1]), imag)
            if step > 0:
                real_term += total[0, :, out]
            imag_term = dot(left(1, spans[0]), real) + dot(left(0, spans[1]), imag)
            if step > 0:
                imag_term += total[1, :, out]
            if step < chips - 1:
                total[0, :, out] = real_term
                total[1, :, out] = imag_term
            else:
                out_ref[0, :, out] = real_term.astype(out_ref.dtype)
                out_ref[1, :, out] = imag_term.astype(out_ref.dtype)

    units = [(step, piece) for step in range(chips) for piece in range(cuts)]
    events = (chips - 1) * cuts
    begin = events // 2
    done = 0
    for event in range(events):
        step, piece = 1 + event // cuts, event % cuts
        for part in range(2):
            hop(part, step - 1, piece).wait_recv()
            if step < chips - 1:
                hop(part, step, piece).start()
            share(part, step, piece).start()
        if event == begin:
            for copy in spread:
                copy.wait_recv()
        if event >= begin:
            goal = min(event + cuts, 3 * (event - begin + 1))
            for unit in units[done:goal]:
                multiply(*unit)
            done = max(done, goal)
    for unit in units[done:]:
        multiply(*unit)

    for copy in spread:
        copy.wait_send()
    for step in range(chips):
        for part, piece in pieces:
            if step < chips - 1:
                hop(part, step, piece).wait_send()
            share(part, step, piece).wait_send()


def solution(mesh):
    bands, rows = mesh.shape["band"], mesh.shape["row"]
    chips = rows // CORES

    def body(coeffs, rotation):
        depth, columns = rotation.shape[1:]
        cuts = max(1, min(4, depth * columns * 2 // PIECE_BYTES))
        tile = min(256, columns // cuts)
        return pl.pallas_call(
            functools.partial(kernel, chips, bands, cuts, tile),
            out_shape=pltpu.VMEM(coeffs.shape, jnp.bfloat16),
            in_specs=[pl.BlockSpec(memory_space=pl.ANY)] * 2,
            out_specs=pl.BlockSpec(memory_space=pltpu.VMEM),
            scratch_shapes=[
                pltpu.VMEM((2, chips, cuts, CORES * depth, columns // cuts), jnp.bfloat16),
                pltpu.VMEM((bands,) + coeffs.shape, jnp.bfloat16),
                pltpu.VMEM(coeffs.shape, jnp.float32),
                pltpu.SemaphoreType.DMA((2, chips - 1, cuts)),
                pltpu.SemaphoreType.DMA((2, chips - 1, cuts)),
                pltpu.SemaphoreType.DMA((2, chips, cuts)),
                pltpu.SemaphoreType.DMA((2, chips, cuts)),
                pltpu.SemaphoreType.DMA((bands - 1,)),
                pltpu.SemaphoreType.DMA((bands - 1,)),
                pltpu.SemaphoreType.DMA((1 + 2 * cuts,)),
            ],
            compiler_params=pltpu.CompilerParams(
                collective_id=0, has_side_effects=True, vmem_limit_bytes=54 * 1024 * 1024
            ),
        )(coeffs, rotation)

    in_specs = (P(None, "row", "band"), P(None, "row", "band"))
    out_specs = P(None, "row", "band")
    return jax.shard_map(body, mesh=mesh, in_specs=in_specs, out_specs=out_specs, check_vma=False)
```
